32 devices in a mesh: dp: 8 (over z, x), expert: 4 (over y, core).
Axes of the slice: x: 2, y: 2, z: 4, core: 2. Of those that a mesh axis runs over, the one named last changes fastest.
Arguments:
- residual: bfloat16 [32, 4096], P(('dp', 'expert')), may hold values from -6 to 6
- norm_gain: float32 [4096], replicated, may hold values from 0.5 to 1.5
- w_gate: bfloat16 [8, 4096, 9216], P('expert', None, 'dp'), may hold values from -0.09375 to 0.09375
- w_up: bfloat16 [8, 4096, 9216], P('expert', None, 'dp'), may hold values from -0.09375 to 0.09375
- w_down: bfloat16 [8, 9216, 4096], P('expert', 'dp'), may hold values from -0.0625 to 0.0625
- routes: int32 [32, 2], P(('dp', 'expert')), may hold values from 0 to 7, all different within a row; in each aligned block of 4 rows (0 to 3, 4 to 7, ...) at most 2 rows name the same one
- gate_weights: float32 [32, 2], P(('dp', 'expert')), may hold values from 0.2 to 1
- valid_mask: int32 [32], P(('dp', 'expert')), may hold values 0 or 1
- keep_group: int32 [8], P('dp'), may hold values 0 or 1
- grad_out: bfloat16 [32, 4096], P(('dp', 'expert')), may hold values from -64 to 64
Outputs:
- grad_residual: float32 [32, 4096], P(('dp', 'expert'))
- gain_update: float32 [4096], replicated
- gate_update: bfloat16 [8, 4096, 9216], P('expert', None, 'dp')
- up_update: bfloat16 [8, 4096, 9216], P('expert', None, 'dp')
- down_update: bfloat16 [8, 9216, 4096], P('expert', 'dp')
The draws below stay inside these ranges and needn't reach their ends.
Inputs may be any that keep to these rules, and one draw needn't show every extreme that they name: `routes`: each row names 2 different experts. In each aligned block of 4 rows (one data group's tokens) no expert is named by more than 2 rows, and in every draw some expert is named by exactly 2 rows of some block.
All inputs are finite; a program needn't handle non-finite values. No bound on the sum of `valid_mask` or of `keep_group` on one device may be relied on, other than what follows from the above.
Results may differ from the reference program's by a relative error of at most 0.0072.
Values may be sent and summed in bfloat16 or wider, within the bound.
A program may use at most 320 MiB of HBM per device.

```python
import math
import jax
import jax.numpy as jnp
import numpy as np
from jax import lax

D = 4096
FF = 9216
NE = 8
TOP = 2
TOK_DEV = 1
CAP = 2
TOKENS = 32
N_DP = 8
N_EXPERT = 4


def plant(result, own_key, least, high):
    index_at = [jax.random.randint(jax.random.fold_in(own_key, axis), (), 0, length) for axis, length in enumerate(result.shape)]
    longest = result.shape.index(max(result.shape))
    beside = index_at[:longest] + [(index_at[longest] + 1) % result.shape[longest]] + index_at[longest + 1:]
    return result.at[tuple(index_at)].set(least).at[tuple(beside)].set(high)


def shard_levels(rng, extent, pieces, low, largest):
    def one(axis_at, blocks):
        heights = jax.random.uniform(jax.random.fold_in(jax.random.fold_in(rng, 6), axis_at), (blocks,), jnp.float32, low / len(pieces), largest / len(pieces))
        return jnp.repeat(jnp.exp(heights), extent[axis_at] // blocks).reshape((-1,) + (1,) * (len(extent) - axis_at - 1))

    loudness = one(*pieces[0])
    for cut in pieces[1:]:
        loudness = loudness * one(*cut)
    return loudness


def deal_out(stream_key, own, number, rows, count, top, bound, skew):
    sequence = jax.random.permutation(stream_key, count)
    heavy_load, common = portions_of(count, rows * top, bound, skew, True), portions_of(count, rows * top, bound, skew, False)
    places = jnp.arange(count)

    def named(tallies, turn):
        used = int((tallies > 0).sum())
        fixed = max(1, used // 4)
        moved = fixed + (places - fixed + turn * (used - fixed)) % max(1, count - fixed)
        return jnp.zeros((count,), jnp.int32).at[sequence[jnp.where(places < fixed, places, moved)]].set(jnp.asarray(tallies, jnp.int32))

    tallies = jnp.where(number % 4 == 0, named(heavy_load, number // 4), named(common, number - number // 4 - 1))
    mixed = jax.random.permutation(jax.random.fold_in(own, 3), count)
    giver, sink = mixed[0:count // 2 * 2:2], mixed[1:count // 2 * 2:2]
    margin = jnp.minimum(tallies[giver] - 1, bound - tallies[sink]) // 2
    margin = jnp.where((giver == sequence[0]) | (sink == sequence[0]) | (tallies[sink] == 0), 0, jnp.maximum(margin, 0))
    moved = jax.random.randint(jax.random.fold_in(own, 4), (count // 2,), 0, 1 << 20) % (margin + 1)
    tallies = tallies.at[giver].add(-moved).at[sink].add(moved)
    labels = jnp.searchsorted(jnp.cumsum(tallies), jnp.arange(rows * top), side="right").astype(jnp.int32)
    table = labels.reshape(top, rows).T
    table = table[jax.random.permutation(jax.random.fold_in(own, 1), rows)]
    turn = jax.random.randint(jax.random.fold_in(own, 2), (rows, 1), 0, top)
    return jnp.take_along_axis(table, (jnp.arange(top)[None, :] + turn) % top, axis=1)


def portions_of(amount, total, most, skew, full):
    weights = [(1 << 20) // math.isqrt(rank ** skew) + 1 for rank in range(1, amount + 1)]
    largest = most if full else min(most, max(-(-total // amount), total * weights[0] // sum(weights)))
    least = 1 if total - largest >= amount - 1 else 0
    holding, surplus = [largest] + [least] * (amount - 1), total - largest - least * (amount - 1)
    while surplus > 0:
        movable = [i for i in range(1, amount) if holding[i] < largest] or [i for i in range(1, amount) if holding[i] < most]
        whole, remaining = sum([weights[i] for i in movable]), surplus
        for i in movable:
            extra = min(most - holding[i], max(1, remaining * weights[i] // whole), surplus)
            holding[i] = holding[i] + extra
            surplus = surplus - extra
    return np.array(holding)


def centred(stream_key, extent, deviation, most, pieces=(), kind=jnp.bfloat16):
    result = jax.random.normal(stream_key, extent, jnp.float32) * deviation
    if len(pieces) > 0:
        result = shard_levels(stream_key, extent, pieces, -0.22, 0.18) * result
    return jnp.clip(result, min=-most, max=most).astype(kind)


def setup_inputs(seed: int = 0) -> dict:
    streams_of = jax.random.split(jax.random.key(seed), 11)
    residual = centred(streams_of[0], (TOKENS, D), 1.0, 6.0, ((0, 32),))
    norm_gain = jnp.clip(1.0 + 0.1 * jax.random.normal(streams_of[1], (D,), jnp.float32), 0.5, 1.5)
    w_gate = centred(streams_of[2], (NE, D, FF), D ** -0.5, 0.09375, ((0, 4), (2, 8)))
    w_up = centred(streams_of[3], (NE, D, FF), D ** -0.5, 0.09375, ((0, 4), (2, 8)))
    w_down = centred(streams_of[4], (NE, FF, D), FF ** -0.5, 0.0625, ((0, 4), (1, 8)))
    routes_keys = jax.random.split(jax.random.fold_in(streams_of[5], 1), TOKENS // (N_EXPERT * TOK_DEV))
    routes_turns = jax.random.permutation(jax.random.fold_in(streams_of[5], 3), TOKENS // (N_EXPERT * TOK_DEV))
    routes = jax.vmap(lambda own, number: deal_out(jax.random.fold_in(streams_of[5], 2), own, number, N_EXPERT * TOK_DEV, NE, TOP, CAP, 2))(routes_keys, routes_turns).reshape((TOKENS, TOP))
    gate_weights = jnp.clip(0.2 + 0.8 * jax.random.uniform(streams_of[6], (TOKENS, TOP), jnp.float32) ** shard_levels(streams_of[6], (TOKENS, TOP), ((0, 32),), -0.2, 0.2), 0.2, 1.0)
    valid_mask = plant((jax.random.randint(streams_of[7], (TOKENS,), 0, 4) < 3).astype(jnp.int32), jax.random.fold_in(streams_of[7], 1), 0, 1)
    keep_group = plant((jax.random.randint(streams_of[8], (N_DP,), 0, 2) < 1).astype(jnp.int32), jax.random.fold_in(streams_of[8], 1), 0, 1)
    grad_out = centred(streams_of[9], (TOKENS, D), (TOKENS // 3), 64.0, ((0, 32),))
    return dict(residual=residual, norm_gain=norm_gain, w_gate=w_gate, w_up=w_up, w_down=w_down, routes=routes, gate_weights=gate_weights, valid_mask=valid_mask, keep_group=keep_group, grad_out=grad_out)


norm_eps = 1e-05

def expert_rows(expert_id, routes, gate_weights):
    hits = routes == expert_id
    weight = lax.optimization_barrier(jnp.sum(jnp.where(hits, gate_weights, jnp.zeros_like(gate_weights)), axis=1))
    flagged = jnp.any(hits, axis=1)
    order = jnp.argsort(jnp.where(flagged, 0, 1).astype(jnp.int32), stable=True)
    return (order[:N_DP * CAP].astype(jnp.int32), weight)

def expert_math(inputs, cotangent, gate_mat, up_mat, down_mat):
    gate_pre = jnp.dot(inputs, gate_mat, preferred_element_type=jnp.float32)
    up_pre = jnp.dot(inputs, up_mat, preferred_element_type=jnp.float32)
    sigma = jax.nn.sigmoid(gate_pre)
    active = gate_pre * sigma
    hidden = (active * up_pre).astype(jnp.bfloat16)
    back_h = jnp.dot(cotangent, down_mat.T, preferred_element_type=jnp.float32)
    d_up = (back_h * active).astype(jnp.bfloat16)
    d_gate = (back_h * up_pre * sigma * (1.0 + gate_pre * (1.0 - sigma))).astype(jnp.bfloat16)
    grad_gate = jnp.dot(inputs.T, d_gate, preferred_element_type=jnp.float32)
    grad_up = jnp.dot(inputs.T, d_up, preferred_element_type=jnp.float32)
    grad_down = jnp.dot(hidden.T, cotangent, preferred_element_type=jnp.float32)
    return (grad_gate, grad_up, grad_down, d_gate, d_up)

def reference(residual, norm_gain, w_gate, w_up, w_down, routes, gate_weights, valid_mask, keep_group, grad_out):
    wide = residual.astype(jnp.float32)
    inv_rms = lax.rsqrt(lax.optimization_barrier(jnp.mean(wide * wide, axis=1, keepdims=True)) + norm_eps)
    normed = wide * inv_rms
    normed_in = (normed * norm_gain).astype(jnp.bfloat16)
    group_of = (jnp.arange(TOKENS) // (TOK_DEV * N_EXPERT)).astype(jnp.int32)
    live = valid_mask * keep_group[group_of]
    count = jnp.maximum(jnp.sum(live).astype(jnp.float32), 1.0)
    masked_grad = jnp.where(live[:, None] > 0, grad_out, jnp.zeros_like(grad_out))

    def pick(expert_id):
        order, weight = expert_rows(expert_id, routes, gate_weights)
        inputs = normed_in[order]
        cotangent = (weight[order][:, None] * masked_grad[order].astype(jnp.float32)).astype(jnp.bfloat16)
        return (order, inputs, cotangent)

    def first_pass(carry, expert_id):
        back_sum, squares = carry
        order, inputs, cotangent = pick(expert_id)
        gate_mat = w_gate[expert_id]
        up_mat = w_up[expert_id]
        grad_gate, grad_up, grad_down, d_gate, d_up = expert_math(inputs, cotangent, gate_mat, up_mat, w_down[expert_id])
        back_x = jnp.dot(d_gate, gate_mat.T, preferred_element_type=jnp.float32) + jnp.dot(d_up, up_mat.T, preferred_element_type=jnp.float32)
        squares = squares + jnp.sum(grad_gate * grad_gate) + jnp.sum(grad_up * grad_up) + jnp.sum(grad_down * grad_down)
        back_sum = back_sum.at[order].add(back_x)
        return ((back_sum, squares), None)
    start = (jnp.zeros((TOKENS, D), jnp.float32), jnp.zeros((), jnp.float32))
    (back_in, squares), _ = lax.scan(first_pass, start, jnp.arange(NE, dtype=jnp.int32))
    gain_grad = lax.optimization_barrier(jnp.sum(back_in * normed, axis=0)) / count
    back_n = back_in * norm_gain
    grad_residual = inv_rms * (back_n - normed * lax.optimization_barrier(jnp.mean(back_n * normed, axis=1, keepdims=True))) / count
    total = squares / (count * count) + jnp.sum(gain_grad * gain_grad)
    param_total = float(3 * NE * D * FF + D)
    factor = 1.0 / jnp.maximum(jnp.sqrt(total / param_total), 1.0)
    scale = factor / count

    def second_pass(expert_id):
        order, inputs, cotangent = pick(expert_id)
        grad_gate, grad_up, grad_down, d_gate, d_up = expert_math(inputs, cotangent, w_gate[expert_id], w_up[expert_id], w_down[expert_id])
        return ((grad_gate * scale).astype(jnp.bfloat16), (grad_up * scale).astype(jnp.bfloat16), (grad_down * scale).astype(jnp.bfloat16))
    gate_update, up_update, down_update = lax.map(second_pass, jnp.arange(NE, dtype=jnp.int32))
    return (grad_residual, gain_grad * factor, gate_update, up_update, down_update)
```

```python
import functools

import jax
import jax.numpy as jnp
from jax import lax
from jax.experimental import pallas as pl
from jax.experimental.pallas import tpu as pltpu
from jax.sharding import PartitionSpec as P

D = 4096
FF = 9216
NE = 8
CAP = 2


norm_eps = 1e-05


def shards_plain(
    residual,
    norm_gain,
    w_gate,
    w_up,
    w_down,
    routes,
    gate_weights,
    valid_mask,
    keep_group,
    grad_out,
):
    wide = residual.astype(jnp.float32)
    inv_rms = lax.rsqrt(jnp.mean(wide * wide, axis=1, keepdims=True) + norm_eps)
    normed = wide * inv_rms
    normed_in = (normed * norm_gain).astype(jnp.bfloat16)
    live = valid_mask * keep_group[0]
    local_count = jnp.sum(live).astype(jnp.float32)
    masked_grad = jnp.where(live[:, None] > 0, grad_out, jnp.zeros_like(grad_out))
    peers = lax.axis_size("expert")
    per_dev = w_gate.shape[0]
    tok_rows = residual.shape[0]
    width = residual.shape[1]
    expert_ids = jnp.arange(peers * per_dev, dtype=jnp.int32).reshape(peers, per_dev)
    hits = routes[None, None, :, :] == expert_ids[:, :, None, None]
    weight = jnp.sum(jnp.where(hits, gate_weights[None, None], jnp.zeros((), jnp.float32)), axis=3)
    flagged = jnp.any(hits, axis=3)
    send_in = jnp.where(flagged[..., None], normed_in[None, None], jnp.zeros((), jnp.bfloat16))
    send_grad = (weight[..., None] * masked_grad[None, None].astype(jnp.float32)).astype(
        jnp.bfloat16
    )
    send_flag = flagged.astype(jnp.bfloat16)
    got_in, got_grad, got_flag = (
        lax.all_to_all(send_in, "expert", split_axis=0, concat_axis=0, tiled=True),
        lax.all_to_all(send_grad, "expert", split_axis=0, concat_axis=0, tiled=True),
        lax.all_to_all(send_flag, "expert", split_axis=0, concat_axis=0, tiled=True),
    )
    group_rows = peers * tok_rows
    cand_in = jnp.transpose(got_in, (1, 0, 2, 3)).reshape(per_dev, group_rows, width)
    cand_grad = jnp.transpose(got_grad, (1, 0, 2, 3)).reshape(per_dev, group_rows, width)
    flag_rows = jnp.transpose(got_flag, (1, 0, 2)).reshape(per_dev, group_rows).astype(jnp.int32)
    ranks = jnp.cumsum(flag_rows, axis=1) - flag_rows
    slot_ids = jnp.arange(CAP, dtype=jnp.int32)
    picker = ((flag_rows[:, None, :] > 0) & (ranks[:, None, :] == slot_ids[None, :, None])).astype(
        jnp.bfloat16
    )
    rows_in = jnp.einsum(
        "lcq,lqd->cld", picker, cand_in, preferred_element_type=jnp.float32
    ).astype(jnp.bfloat16)
    rows_grad = jnp.einsum(
        "lcq,lqd->cld", picker, cand_grad, preferred_element_type=jnp.float32
    ).astype(jnp.bfloat16)
    all_in, all_grad = (
        lax.all_gather(rows_in, "dp", axis=0, tiled=True),
        lax.all_gather(rows_grad, "dp", axis=0, tiled=True),
    )
    gate_pre = jnp.einsum("rld,ldf->rlf", all_in, w_gate, preferred_element_type=jnp.float32)
    up_pre = jnp.einsum("rld,ldf->rlf", all_in, w_up, preferred_element_type=jnp.float32)
    sigma = jax.nn.sigmoid(gate_pre)
    active = gate_pre * sigma
    hidden = (active * up_pre).astype(jnp.bfloat16)
    back_h = jnp.einsum("rld,lfd->rlf", all_grad, w_down, preferred_element_type=jnp.float32)
    d_up = (back_h * active).astype(jnp.bfloat16)
    d_gate = (back_h * up_pre * sigma * (1.0 + gate_pre * (1.0 - sigma))).astype(jnp.bfloat16)
    grad_gate = jnp.einsum("rld,rlf->ldf", all_in, d_gate, preferred_element_type=jnp.float32)
    grad_up = jnp.einsum("rld,rlf->ldf", all_in, d_up, preferred_element_type=jnp.float32)
    grad_down = jnp.einsum("rlf,rld->lfd", hidden, all_grad, preferred_element_type=jnp.float32)
    first = jnp.einsum("rlf,ldf->rld", d_gate, w_gate, preferred_element_type=jnp.float32)
    back_mine = lax.psum_scatter(
        first + jnp.einsum("rlf,ldf->rld", d_up, w_up, preferred_element_type=jnp.float32),
        "dp",
        scatter_dimension=0,
        tiled=True,
    )
    back_cand = jnp.einsum(
        "lcq,cld->lqd", picker.astype(jnp.float32), back_mine, precision=lax.Precision.HIGHEST
    )
    back_send = jnp.transpose(back_cand.reshape(per_dev, peers, tok_rows, width), (1, 0, 2, 3))
    back_got = lax.all_to_all(back_send, "expert", split_axis=0, concat_axis=0, tiled=True)
    back_in = jnp.sum(back_got, axis=(0, 1))
    gain_local = jnp.sum(back_in * normed, axis=0)
    back_n = back_in * norm_gain
    grad_core = inv_rms * (back_n - normed * jnp.mean(back_n * normed, axis=1, keepdims=True))
    param_total = float(3 * NE * D * FF + D)
    local_sq = (
        jnp.sum(grad_gate * grad_gate) + jnp.sum(grad_up * grad_up) + jnp.sum(grad_down * grad_down)
    )
    count_all, gain_all, squares_all = lax.psum(
        (local_count, gain_local, local_sq), ("dp", "expert")
    )
    count = jnp.maximum(count_all, 1.0)
    gain_grad = gain_all / count
    total = squares_all / (count * count) + jnp.sum(gain_grad * gain_grad)
    factor = 1.0 / jnp.maximum(jnp.sqrt(total / param_total), 1.0)
    scale = factor / count
    grad_residual = grad_core / count
    gate_update = (grad_gate * scale).astype(jnp.bfloat16)
    up_update = (grad_up * scale).astype(jnp.bfloat16)
    down_update = (grad_down * scale).astype(jnp.bfloat16)
    return (grad_residual, gain_grad * factor, gate_update, up_update, down_update)


MESH = pl.DeviceIdType.MESH
VMEM = pl.BlockSpec(memory_space=pltpu.VMEM)
NT = (((1,), (1,)), ((), ()))
TN = (((0,), (0,)), ((), ()))


def peer_at(n_expert, index):
    return (index // n_expert, index % n_expert)


def greet(n, n_expert, me):
    barrier = pltpu.get_barrier_semaphore()

    def hello(k, _):
        peer = (me + k) % n
        pl.semaphore_signal(
            barrier, inc=1, device_id=peer_at(n_expert, peer), device_id_type=MESH
        )
        return 0

    lax.fori_loop(1, n, hello, 0)
    pl.semaphore_wait(barrier, n - 1)


def exchange(n, n_expert, me, source, land, send_sem, recv_sem):
    def copy_to(peer):
        return pltpu.make_async_remote_copy(
            src_ref=source(peer),
            dst_ref=land.at[me],
            send_sem=send_sem.at[peer],
            recv_sem=recv_sem.at[me],
            device_id=peer_at(n_expert, peer),
            device_id_type=MESH,
        )

    def start(k, _):
        copy_to((me + k) % n).start()
        return 0

    lax.fori_loop(1, n, start, 0)

    def wait_recv():
        def one(k, _):
            peer = (me + k) % n
            pltpu.make_async_remote_copy(
                src_ref=source(peer),
                dst_ref=land.at[peer],
                send_sem=send_sem.at[peer],
                recv_sem=recv_sem.at[peer],
                device_id=peer_at(n_expert, peer),
                device_id_type=MESH,
            ).wait_recv()
            return 0

        lax.fori_loop(1, n, one, 0)

    def wait_send():
        def one(k, _):
            copy_to((me + k) % n).wait_send()
            return 0

        lax.fori_loop(1, n, one, 0)

    return wait_recv, wait_send


def gather_kernel(n, n_expert, rows_ref, meta_ref, rows_out, meta_out, land_rows, land_meta, sems):
    me = lax.axis_index("dp") * n_expert + lax.axis_index("expert")
    greet(n, n_expert, me)
    rows_recv, rows_send = exchange(
        n, n_expert, me, lambda peer: rows_ref, land_rows, sems.at[0], sems.at[1]
    )
    meta_recv, meta_send = exchange(
        n, n_expert, me, lambda peer: meta_ref, land_meta, sems.at[2], sems.at[3]
    )
    land_rows[me] = rows_ref[...]
    land_meta[me] = meta_ref[...]
    rows_recv()
    meta_recv()
    rows_out[...] = land_rows[...]
    meta_out[...] = land_meta[...]
    rows_send()
    meta_send()


def expert_kernel(
    n_tiles,
    res_ref,
    grad_ref,
    meta_ref,
    gain_ref,
    wg_ref,
    wu_ref,
    wd_ref,
    x_out,
    c_out,
    dg_out,
    du_out,
    h_out,
    back_out,
    gainp_out,
    sq_out,
    normed,
    gram,
    gram_h,
):
    l, f = pl.program_id(0), pl.program_id(1)
    per_dev = pl.num_programs(0)

    @pl.when((l == 0) & (f == 0))
    def _():
        wide = res_ref[...].astype(jnp.float32)
        inv_rms = lax.rsqrt(jnp.mean(wide * wide, axis=1, keepdims=True) + norm_eps)
        normed[...] = wide * inv_rms
        x_out[...] = (normed[...] * gain_ref[...]).astype(jnp.bfloat16)
        back_out[...] = jnp.zeros_like(back_out)
        sq_out[...] = jnp.zeros_like(sq_out)

    @pl.when(f == 0)
    def _():
        own = (lax.axis_index("expert") * per_dev + l).astype(jnp.float32)
        meta = meta_ref[...]
        weight = jnp.where(meta[:, 0:1] == own, meta[:, 2:3], 0.0) + jnp.where(
            meta[:, 1:2] == own, meta[:, 3:4], 0.0
        )
        masked = jnp.where(meta[:, 4:5] > 0, grad_ref[...].astype(jnp.float32), 0.0)
        c_out[0] = (weight * masked).astype(jnp.bfloat16)
        gram[...] = jnp.zeros_like(gram)
        gram_h[...] = jnp.zeros_like(gram_h)

    x = x_out[...]
    c = c_out[0]
    f32 = dict(preferred_element_type=jnp.float32)
    gate_pre = jnp.dot(x, wg_ref[0], **f32)
    up_pre = jnp.dot(x, wu_ref[0], **f32)
    back_h = lax.dot_general(c, wd_ref[0], NT, **f32)
    sigma = jax.nn.sigmoid(gate_pre)
    active = gate_pre * sigma
    hidden = (active * up_pre).astype(jnp.bfloat16)
    d_up = (back_h * active).astype(jnp.bfloat16)
    d_gate = (back_h * up_pre * sigma * (1.0 + gate_pre * (1.0 - sigma))).astype(jnp.bfloat16)
    dg_out[0] = d_gate
    du_out[0] = d_up
    h_out[0] = hidden
    back_out[...] += lax.dot_general(d_gate, wg_ref[0], NT, **f32) + lax.dot_general(
        d_up, wu_ref[0], NT, **f32
    )
    gram[...] += lax.dot_general(d_gate, d_gate, NT, **f32) + lax.dot_general(
        d_up, d_up, NT, **f32
    )
    gram_h[...] += lax.dot_general(hidden, hidden, NT, **f32)

    @pl.when(f == n_tiles - 1)
    def _():
        terms = gram[...] * lax.dot_general(x, x, NT, **f32) + gram_h[...] * lax.dot_general(
            c, c, NT, **f32
        )
        sq_out[...] += jnp.sum(terms)

    @pl.when((l == per_dev - 1) & (f == n_tiles - 1))
    def _():
        gainp_out[...] = jnp.sum(back_out[...] * normed[...], axis=0, keepdims=True)


def reduce_kernel(
    n, n_expert, small_ref, back_ref, small_out, gain_out, back_sum, land_small, part, land_gain, land_back, sems
):
    me = lax.axis_index("dp") * n_expert + lax.axis_index("expert")
    greet(n, n_expert, me)
    small_recv, small_send = exchange(
        n, n_expert, me, lambda peer: small_ref.at[peer], land_small, sems.at[0], sems.at[1]
    )
    land_small[me] = small_ref[me]
    small_recv()
    total = jnp.sum(land_small[...], axis=0)
    small_out[...] = total
    part[...] = total[0:1]
    gain_recv, gain_send = exchange(
        n, n_expert, me, lambda peer: part, land_gain, sems.at[2], sems.at[3]
    )
    land_gain[me] = part[...]
    back_recv, back_send = exchange(
        n, n_expert, me, lambda peer: back_ref.at[peer], land_back, sems.at[4], sems.at[5]
    )
    land_back[me] = back_ref[me]
    gain_recv()
    gain_out[...] = land_gain[...]
    back_recv()
    back_sum[...] = jnp.sum(land_back[...], axis=0)
    small_send()
    gain_send()
    back_send()


def update_kernel(x_ref, c_ref, dg_ref, du_ref, h_ref, scale_ref, og_ref, ou_ref, od_ref, xt):
    @pl.when((pl.program_id(0) == 0) & (pl.program_id(1) == 0))
    def _():
        xt[...] = x_ref[...].T

    scale = scale_ref[0]
    f32 = dict(preferred_element_type=jnp.float32)
    og_ref[0] = (jnp.dot(xt[...], dg_ref[0], **f32) * scale).astype(jnp.bfloat16)
    ou_ref[0] = (jnp.dot(xt[...], du_ref[0], **f32) * scale).astype(jnp.bfloat16)
    od_ref[0] = (lax.dot_general(h_ref[0], c_ref[0], TN, **f32) * scale).astype(jnp.bfloat16)


def shards_kernel(
    n_dp,
    n_expert,
    residual,
    norm_gain,
    w_gate,
    w_up,
    w_down,
    routes,
    gate_weights,
    valid_mask,
    keep_group,
    grad_out,
):
    n = n_dp * n_expert
    per_dev, width, hid = w_gate.shape
    lanes = width // 128
    live = (valid_mask * keep_group[0])[:, None].astype(jnp.float32)
    meta = jnp.concatenate([routes.astype(jnp.float32), gate_weights, live], axis=1)
    meta = jnp.pad(meta, ((0, 0), (0, 128 - meta.shape[1])))
    rows = jnp.concatenate([residual, grad_out], axis=0).reshape(2, lanes, 128)
    big = dict(vmem_limit_bytes=60000 * 1024)
    rows_all, meta_all = pl.pallas_call(
        functools.partial(gather_kernel, n, n_expert),
        out_shape=(
            jax.ShapeDtypeStruct((n, 2, lanes, 128), jnp.bfloat16),
            jax.ShapeDtypeStruct((n, 1, 128), jnp.float32),
        ),
        in_specs=[VMEM] * 2,
        out_specs=[VMEM] * 2,
        scratch_shapes=[
            pltpu.VMEM((n, 2, lanes, 128), jnp.bfloat16),
            pltpu.VMEM((n, 1, 128), jnp.float32),
            pltpu.SemaphoreType.DMA((4, n)),
        ],
        compiler_params=pltpu.CompilerParams(collective_id=0, has_side_effects=True),
        name="gather_rows",
    )(rows, meta)
    res_all = rows_all[:, 0].reshape(n, width)
    grad_all = rows_all[:, 1].reshape(n, width)
    meta_all = meta_all.reshape(n, 128)
    tile = next(t for t in (384, 256, 128) if hid % t == 0)
    n_tiles = hid // tile
    hidden_shape = jax.ShapeDtypeStruct((per_dev, n, hid), jnp.bfloat16)
    whole = lambda *shape: pl.BlockSpec(shape, lambda l, f: (0,) * len(shape))
    col = lambda rows: pl.BlockSpec((1, rows, tile), lambda l, f: (l, 0, f))
    row = lambda cols: pl.BlockSpec((1, tile, cols), lambda l, f: (l, f, 0))
    per_expert = pl.BlockSpec((1, n, width), lambda l, f: (l, 0, 0))
    x, c, d_gate, d_up, hidden, back, gain_part, squares = pl.pallas_call(
        functools.partial(expert_kernel, n_tiles),
        grid=(per_dev, n_tiles),
        out_shape=(
            jax.ShapeDtypeStruct((n, width), jnp.bfloat16),
            jax.ShapeDtypeStruct((per_dev, n, width), jnp.bfloat16),
            hidden_shape,
            hidden_shape,
            hidden_shape,
            jax.ShapeDtypeStruct((n, width), jnp.float32),
            jax.ShapeDtypeStruct((1, width), jnp.float32),
            jax.ShapeDtypeStruct((1, 128), jnp.float32),
        ),
        in_specs=[
            whole(n, width),
            whole(n, width),
            whole(n, 128),
            whole(1, width),
            col(width),
            col(width),
            row(width),
        ],
        out_specs=[
            whole(n, width),
            per_expert,
            col(n),
            col(n),
            col(n),
            whole(n, width),
            whole(1, width),
            whole(1, 128),
        ],
        scratch_shapes=[
            pltpu.VMEM((n, width), jnp.float32),
            pltpu.VMEM((n, n), jnp.float32),
            pltpu.VMEM((n, n), jnp.float32),
        ],
        compiler_params=pltpu.CompilerParams(**big),
        name="expert_pass",
    )(res_all, grad_all, meta_all, norm_gain[None], w_gate, w_up, w_down)
    small = jnp.concatenate(
        [gain_part.reshape(n, 1, width // n), jnp.broadcast_to(squares[None], (n, 1, width // n))],
        axis=1,
    )
    small_sum, gain_all, back_in = pl.pallas_call(
        functools.partial(reduce_kernel, n, n_expert),
        out_shape=(
            jax.ShapeDtypeStruct((2, width // n), jnp.float32),
            jax.ShapeDtypeStruct((n, 1, width // n), jnp.float32),
            jax.ShapeDtypeStruct((lanes, 128), jnp.float32),
        ),
        in_specs=[VMEM] * 2,
        out_specs=[VMEM] * 3,
        scratch_shapes=[
            pltpu.VMEM((n, 2, width // n), jnp.float32),
            pltpu.VMEM((1, width // n), jnp.float32),
            pltpu.VMEM((n, 1, width // n), jnp.float32),
            pltpu.VMEM((n, lanes, 128), jnp.float32),
            pltpu.SemaphoreType.DMA((6, n)),
        ],
        compiler_params=pltpu.CompilerParams(collective_id=1, has_side_effects=True),
        name="reduce_rows",
    )(small, back.reshape(n, lanes, 128))
    count = jnp.maximum(jnp.sum(meta_all[:, 4]), 1.0)
    gain_grad = gain_all.reshape(width) / count
    param_total = float(3 * n_expert * per_dev * width * hid * n_dp + width)
    total = small_sum[1, 0] / (count * count) + jnp.sum(gain_grad * gain_grad)
    factor = 1.0 / jnp.maximum(jnp.sqrt(total / param_total), 1.0)
    scale = factor / count
    gate_update, up_update, down_update = pl.pallas_call(
        update_kernel,
        grid=(per_dev, n_tiles),
        out_shape=(
            jax.ShapeDtypeStruct(w_gate.shape, jnp.bfloat16),
            jax.ShapeDtypeStruct(w_up.shape, jnp.bfloat16),
            jax.ShapeDtypeStruct(w_down.shape, jnp.bfloat16),
        ),
        in_specs=[
            whole(n, width),
            per_expert,
            col(n),
            col(n),
            col(n),
            pl.BlockSpec(memory_space=pltpu.SMEM),
        ],
        out_specs=[col(width), col(width), row(width)],
        scratch_shapes=[pltpu.VMEM((width, n), jnp.bfloat16)],
        compiler_params=pltpu.CompilerParams(**big),
        name="update_pass",
    )(x, c, d_gate, d_up, hidden, scale[None])
    wide = residual.astype(jnp.float32)
    inv_rms = lax.rsqrt(jnp.mean(wide * wide, axis=1, keepdims=True) + norm_eps)
    normed = wide * inv_rms
    back_n = back_in.reshape(1, width) * norm_gain
    grad_core = inv_rms * (back_n - normed * jnp.mean(back_n * normed, axis=1, keepdims=True))
    return (grad_core / count, gain_grad * factor, gate_update, up_update, down_update)


def shards_for(mesh):
    n_dp, n_expert = mesh.shape["dp"], mesh.shape["expert"]

    def run(*args):
        residual, w_gate = args[0], args[2]
        width, hid = w_gate.shape[1:]
        n = n_dp * n_expert
        fits = residual.shape[0] == 1 and hid % 128 == 0 and width == n * 128
        if fits:
            return shards_kernel(n_dp, n_expert, *args)
        return shards_plain(*args)

    return run


def solution(mesh):
    placed = (
        P(("dp", "expert"), None),
        P(),
        P("expert", None, "dp"),
        P("expert", None, "dp"),
        P("expert", "dp", None),
        P(("dp", "expert"), None),
        P(("dp", "expert"), None),
        P(("dp", "expert")),
        P("dp"),
        P(("dp", "expert"), None),
    )
    return jax.shard_map(
        shards_for(mesh),
        mesh=mesh,
        in_specs=placed,
        out_specs=(
            P(("dp", "expert"), None),
            P(),
            P("expert", None, "dp"),
            P("expert", None, "dp"),
            P("expert", "dp", None),
        ),
        check_vma=False,
    )
```

```python
import functools

import jax
import jax.numpy as jnp
from jax import lax
from jax.experimental import pallas as pl
from jax.experimental.pallas import tpu as pltpu
from jax.sharding import PartitionSpec as P

D = 4096
FF = 9216
NE = 8
CAP = 2


norm_eps = 1e-05


def shards_plain(
    residual,
    norm_gain,
    w_gate,
    w_up,
    w_down,
    routes,
    gate_weights,
    valid_mask,
    keep_group,
    grad_out,
):
    wide = residual.astype(jnp.float32)
    inv_rms = lax.rsqrt(jnp.mean(wide * wide, axis=1, keepdims=True) + norm_eps)
    normed = wide * inv_rms
    normed_in = (normed * norm_gain).astype(jnp.bfloat16)
    live = valid_mask * keep_group[0]
    local_count = jnp.sum(live).astype(jnp.float32)
    masked_grad = jnp.where(live[:, None] > 0, grad_out, jnp.zeros_like(grad_out))
    peers = lax.axis_size("expert")
    per_dev = w_gate.shape[0]
    tok_rows = residual.shape[0]
    width = residual.shape[1]
    expert_ids = jnp.arange(peers * per_dev, dtype=jnp.int32).reshape(peers, per_dev)
    hits = routes[None, None, :, :] == expert_ids[:, :, None, None]
    weight = jnp.sum(jnp.where(hits, gate_weights[None, None], jnp.zeros((), jnp.float32)), axis=3)
    flagged = jnp.any(hits, axis=3)
    send_in = jnp.where(flagged[..., None], normed_in[None, None], jnp.zeros((), jnp.bfloat16))
    send_grad = (weight[..., None] * masked_grad[None, None].astype(jnp.float32)).astype(
        jnp.bfloat16
    )
    send_flag = flagged.astype(jnp.bfloat16)
    got_in, got_grad, got_flag = (
        lax.all_to_all(send_in, "expert", split_axis=0, concat_axis=0, tiled=True),
        lax.all_to_all(send_grad, "expert", split_axis=0, concat_axis=0, tiled=True),
        lax.all_to_all(send_flag, "expert", split_axis=0, concat_axis=0, tiled=True),
    )
    group_rows = peers * tok_rows
    cand_in = jnp.transpose(got_in, (1, 0, 2, 3)).reshape(per_dev, group_rows, width)
    cand_grad = jnp.transpose(got_grad, (1, 0, 2, 3)).reshape(per_dev, group_rows, width)
    flag_rows = jnp.transpose(got_flag, (1, 0, 2)).reshape(per_dev, group_rows).astype(jnp.int32)
    ranks = jnp.cumsum(flag_rows, axis=1) - flag_rows
    slot_ids = jnp.arange(CAP, dtype=jnp.int32)
    picker = ((flag_rows[:, None, :] > 0) & (ranks[:, None, :] == slot_ids[None, :, None])).astype(
        jnp.bfloat16
    )
    rows_in = jnp.einsum(
        "lcq,lqd->cld", picker, cand_in, preferred_element_type=jnp.float32
    ).astype(jnp.bfloat16)
    rows_grad = jnp.einsum(
        "lcq,lqd->cld", picker, cand_grad, preferred_element_type=jnp.float32
    ).astype(jnp.bfloat16)
    all_in, all_grad = (
        lax.all_gather(rows_in, "dp", axis=0, tiled=True),
        lax.all_gather(rows_grad, "dp", axis=0, tiled=True),
    )
    gate_pre = jnp.einsum("rld,ldf->rlf", all_in, w_gate, preferred_element_type=jnp.float32)
    up_pre = jnp.einsum("rld,ldf->rlf", all_in, w_up, preferred_element_type=jnp.float32)
    sigma = jax.nn.sigmoid(gate_pre)
    active = gate_pre * sigma
    hidden = (active * up_pre).astype(jnp.bfloat16)
    back_h = jnp.einsum("rld,lfd->rlf", all_grad, w_down, preferred_element_type=jnp.float32)
    d_up = (back_h * active).astype(jnp.bfloat16)
    d_gate = (back_h * up_pre * sigma * (1.0 + gate_pre * (1.0 - sigma))).astype(jnp.bfloat16)
    grad_gate = jnp.einsum("rld,rlf->ldf", all_in, d_gate, preferred_element_type=jnp.float32)
    grad_up = jnp.einsum("rld,rlf->ldf", all_in, d_up, preferred_element_type=jnp.float32)
    grad_down = jnp.einsum("rlf,rld->lfd", hidden, all_grad, preferred_element_type=jnp.float32)
    first = jnp.einsum("rlf,ldf->rld", d_gate, w_gate, preferred_element_type=jnp.float32)
    back_mine = lax.psum_scatter(
        first + jnp.einsum("rlf,ldf->rld", d_up, w_up, preferred_element_type=jnp.float32),
        "dp",
        scatter_dimension=0,
        tiled=True,
    )
    back_cand = jnp.einsum(
        "lcq,cld->lqd", picker.astype(jnp.float32), back_mine, precision=lax.Precision.HIGHEST
    )
    back_send = jnp.transpose(back_cand.reshape(per_dev, peers, tok_rows, width), (1, 0, 2, 3))
    back_got = lax.all_to_all(back_send, "expert", split_axis=0, concat_axis=0, tiled=True)
    back_in = jnp.sum(back_got, axis=(0, 1))
    gain_local = jnp.sum(back_in * normed, axis=0)
    back_n = back_in * norm_gain
    grad_core = inv_rms * (back_n - normed * jnp.mean(back_n * normed, axis=1, keepdims=True))
    param_total = float(3 * NE * D * FF + D)
    local_sq = (
        jnp.sum(grad_gate * grad_gate) + jnp.sum(grad_up * grad_up) + jnp.sum(grad_down * grad_down)
    )
    count_all, gain_all, squares_all = lax.psum(
        (local_count, gain_local, local_sq), ("dp", "expert")
    )
    count = jnp.maximum(count_all, 1.0)
    gain_grad = gain_all / count
    total = squares_all / (count * count) + jnp.sum(gain_grad * gain_grad)
    factor = 1.0 / jnp.maximum(jnp.sqrt(total / param_total), 1.0)
    scale = factor / count
    grad_residual = grad_core / count
    gate_update = (grad_gate * scale).astype(jnp.bfloat16)
    up_update = (grad_up * scale).astype(jnp.bfloat16)
    down_update = (grad_down * scale).astype(jnp.bfloat16)
    return (grad_residual, gain_grad * factor, gate_update, up_update, down_update)


MESH = pl.DeviceIdType.MESH
VMEM = pl.BlockSpec(memory_space=pltpu.VMEM)
NT = (((1,), (1,)), ((), ()))
TN = (((0,), (0,)), ((), ()))


def greet(axes):
    barrier = pltpu.get_barrier_semaphore()
    total = 0
    for axis, size in axes.items():
        me = lax.axis_index(axis)
        for k in range(1, size):
            pl.semaphore_signal(
                barrier, inc=1, device_id={axis: (me + k) % size}, device_id_type=MESH
            )
        total += size - 1
    pl.semaphore_wait(barrier, total)


def exchange(axis, size, source, land, send_sem, recv_sem):
    me = lax.axis_index(axis)

    def copy(peer, slot):
        return pltpu.make_async_remote_copy(
            src_ref=source(peer),
            dst_ref=land.at[slot],
            send_sem=send_sem.at[peer],
            recv_sem=recv_sem.at[slot],
            device_id={axis: peer},
            device_id_type=MESH,
        )

    peers = [(me + k) % size for k in range(1, size)]
    for peer in peers:
        copy(peer, me).start()

    def wait_recv():
        for peer in peers:
            copy(peer, peer).wait_recv()

    def wait_send():
        for peer in peers:
            copy(peer, me).wait_send()

    return wait_recv, wait_send


def gather_kernel(
    n_dp, n_expert, res_ref, grad_ref, routes_ref, gates_ref, valid_ref, keep_ref,
    res_out, grad_out, meta_out, land_rows, land_meta, send, recv,
):
    d, e = lax.axis_index("dp"), lax.axis_index("expert")
    lane = lax.broadcasted_iota(jnp.int32, (1, 128), 1)
    parts = (
        routes_ref[:, 0:1].astype(jnp.float32),
        routes_ref[:, 1:2].astype(jnp.float32),
        gates_ref[:, 0:1],
        gates_ref[:, 1:2],
        (valid_ref[...] * keep_ref[...]).astype(jnp.float32),
    )
    meta = jnp.zeros((1, 128), jnp.float32)
    for at, part in enumerate(parts):
        meta = jnp.where(lane == at, part, meta)
    land_rows[d, e, 0] = res_ref[...]
    land_rows[d, e, 1] = grad_ref[...]
    land_meta[d, e] = meta
    greet({"dp": n_dp, "expert": n_expert})
    waits = [
        exchange("expert", n_expert, lambda p, land=land: land.at[d, e], land.at[d], send.at[i], recv.at[i])
        for i, land in enumerate((land_rows, land_meta))
    ]
    for wait in waits:
        wait[0]()
    more = [
        exchange("dp", n_dp, lambda p, land=land: land.at[d], land, send.at[2 + i], recv.at[2 + i])
        for i, land in enumerate((land_rows, land_meta))
    ]
    for wait in more:
        wait[0]()
    res_out[...] = land_rows[:, :, 0]
    grad_out[...] = land_rows[:, :, 1]
    meta_out[...] = land_meta[...]
    for wait in waits + more:
        wait[1]()


def expert_kernel(
    n_tiles,
    res_ref,
    grad_ref,
    meta_ref,
    gain_ref,
    wg_ref,
    wu_ref,
    wd_ref,
    x_out,
    c_out,
    dg_out,
    du_out,
    h_out,
    groups_out,
    gainp_out,
    sq_out,
    normed,
    gram,
    gram_h,
    back_out,
):
    l, f = pl.program_id(0), pl.program_id(1)
    per_dev = pl.num_programs(0)

    @pl.when((l == 0) & (f == 0))
    def _():
        wide = res_ref[...].astype(jnp.float32)
        inv_rms = lax.rsqrt(jnp.mean(wide * wide, axis=1, keepdims=True) + norm_eps)
        normed[...] = wide * inv_rms
        x_out[...] = (normed[...] * gain_ref[...]).astype(jnp.bfloat16)
        back_out[...] = jnp.zeros_like(back_out)
        sq_out[...] = jnp.zeros_like(sq_out)

    @pl.when(f == 0)
    def _():
        own = (lax.axis_index("expert") * per_dev + l).astype(jnp.float32)
        meta = meta_ref[...]
        weight = jnp.where(meta[:, 0:1] == own, meta[:, 2:3], 0.0) + jnp.where(
            meta[:, 1:2] == own, meta[:, 3:4], 0.0
        )
        masked = jnp.where(meta[:, 4:5] > 0, grad_ref[...].astype(jnp.float32), 0.0)
        c_out[0] = (weight * masked).astype(jnp.bfloat16)
        gram[...] = jnp.zeros_like(gram)
        gram_h[...] = jnp.zeros_like(gram_h)

    x = x_out[...]
    c = c_out[0]
    f32 = dict(preferred_element_type=jnp.float32)
    gate_pre = jnp.dot(x, wg_ref[0], **f32)
    up_pre = jnp.dot(x, wu_ref[0], **f32)
    back_h = lax.dot_general(c, wd_ref[0], NT, **f32)
    sigma = jax.nn.sigmoid(gate_pre)
    active = gate_pre * sigma
    hidden = (active * up_pre).astype(jnp.bfloat16)
    d_up = (back_h * active).astype(jnp.bfloat16)
    d_gate = (back_h * up_pre * sigma * (1.0 + gate_pre * (1.0 - sigma))).astype(jnp.bfloat16)
    dg_out[0] = d_gate
    du_out[0] = d_up
    h_out[0] = hidden
    back_out[...] += lax.dot_general(d_gate, wg_ref[0], NT, **f32) + lax.dot_general(
        d_up, wu_ref[0], NT, **f32
    )
    gram[...] += lax.dot_general(d_gate, d_gate, NT, **f32) + lax.dot_general(
        d_up, d_up, NT, **f32
    )
    gram_h[...] += lax.dot_general(hidden, hidden, NT, **f32)

    @pl.when(f == n_tiles - 1)
    def _():
        terms = gram[...] * lax.dot_general(x, x, NT, **f32) + gram_h[...] * lax.dot_general(
            c, c, NT, **f32
        )
        sq_out[...] += jnp.sum(terms)

    @pl.when((l == per_dev - 1) & (f == n_tiles - 1))
    def _():
        size = groups_out.shape[1]
        for k in range(groups_out.shape[0]):
            groups_out[k] = back_out[k * size : (k + 1) * size]
        gainp_out[...] = jnp.sum(back_out[...] * normed[...], axis=0, keepdims=True)


def reduce_kernel(
    n_dp, n_expert, param_total, gainp_ref, sq_ref, back_ref, meta_ref, res_ref, gain_ref,
    resid_out, gain_out, scale_out,
    msg, land_msg, land_part, land_gain, land_back, stage, land_row, send, recv,
):
    d, e = lax.axis_index("dp"), lax.axis_index("expert")
    piece = gainp_ref.shape[1] // n_dp
    for k in range(n_dp):
        msg[k, :, :piece] = gainp_ref[:, k * piece : (k + 1) * piece]
        msg[k, :, piece:] = sq_ref[...]
    greet({"dp": n_dp, "expert": n_expert})
    first = exchange("dp", n_dp, lambda p: msg.at[p], land_msg, send.at[0], recv.at[0])
    land_msg[d] = msg[d]
    back = exchange("dp", n_dp, lambda p: back_ref.at[p], land_back, send.at[3], recv.at[3])
    land_back[d] = back_ref[d]
    first[0]()
    land_part[e] = jnp.sum(land_msg[...], axis=0)
    second = exchange(
        "expert", n_expert, lambda p: land_part.at[e], land_part, send.at[1], recv.at[1]
    )
    second[0]()
    total = jnp.sum(land_part[...], axis=0)
    land_gain[d] = total[:, :piece]
    third = exchange("dp", n_dp, lambda p: land_gain.at[d], land_gain, send.at[2], recv.at[2])
    back[0]()
    group = jnp.sum(land_back[...], axis=0)
    for k in range(n_expert):
        stage[k] = group[k : k + 1]
    last = exchange("expert", n_expert, lambda p: stage.at[p], land_row, send.at[4], recv.at[4])
    land_row[e] = stage[e]
    third[0]()
    count = jnp.maximum(jnp.sum(meta_ref[:, :, :, 4:5]), 1.0)
    gain_grad = land_gain[...] / count
    whole = total[:, piece : piece + 1] / (count * count) + jnp.sum(gain_grad * gain_grad)
    factor = 1.0 / jnp.maximum(jnp.sqrt(whole / param_total), 1.0)
    gain_out[...] = gain_grad * factor
    scale_out[...] = jnp.broadcast_to(factor / count, scale_out.shape)
    wide = res_ref[...].astype(jnp.float32)
    inv_rms = lax.rsqrt(jnp.mean(wide * wide, axis=1, keepdims=True) + norm_eps)
    normed = wide * inv_rms
    last[0]()
    back_n = jnp.sum(land_row[...], axis=0) * gain_ref[...]
    core = inv_rms * (back_n - normed * jnp.mean(back_n * normed, axis=1, keepdims=True))
    resid_out[...] = core / count
    for wait in (first, second, third, back, last):
        wait[1]()


def update_kernel(x_ref, c_ref, dg_ref, du_ref, h_ref, scale_ref, og_ref, ou_ref, od_ref, xt):
    @pl.when((pl.program_id(0) == 0) & (pl.program_id(1) == 0))
    def _():
        xt[...] = x_ref[...].T

    scale = scale_ref[:, 0:1]
    f32 = dict(preferred_element_type=jnp.float32)
    og_ref[0] = (jnp.dot(xt[...], dg_ref[0], **f32) * scale).astype(jnp.bfloat16)
    ou_ref[0] = (jnp.dot(xt[...], du_ref[0], **f32) * scale).astype(jnp.bfloat16)
    od_ref[0] = (lax.dot_general(h_ref[0], c_ref[0], TN, **f32) * scale).astype(jnp.bfloat16)


def shards_kernel(
    n_dp,
    n_expert,
    residual,
    norm_gain,
    w_gate,
    w_up,
    w_down,
    routes,
    gate_weights,
    valid_mask,
    keep_group,
    grad_out,
):
    n = n_dp * n_expert
    per_dev, width, hid = w_gate.shape
    lanes = width // 128
    big = dict(vmem_limit_bytes=60000 * 1024)
    most = max(n_dp, n_expert)
    rows_shape = jax.ShapeDtypeStruct((n_dp, n_expert, lanes, 128), jnp.bfloat16)
    res_all, grad_all, meta_all = pl.pallas_call(
        functools.partial(gather_kernel, n_dp, n_expert),
        out_shape=(
            rows_shape,
            rows_shape,
            jax.ShapeDtypeStruct((n_dp, n_expert, 1, 128), jnp.float32),
        ),
        in_specs=[VMEM] * 6,
        out_specs=[VMEM] * 3,
        scratch_shapes=[
            pltpu.VMEM((n_dp, n_expert, 2, lanes, 128), jnp.bfloat16),
            pltpu.VMEM((n_dp, n_expert, 1, 128), jnp.float32),
            pltpu.SemaphoreType.DMA((4, most)),
            pltpu.SemaphoreType.DMA((4, most)),
        ],
        compiler_params=pltpu.CompilerParams(collective_id=0, has_side_effects=True),
        name="gather_rows",
    )(
        residual.reshape(lanes, 128),
        grad_out.reshape(lanes, 128),
        routes,
        gate_weights,
        valid_mask[None],
        keep_group[None],
    )
    tile = next(t for t in (384, 256, 128) if hid % t == 0)
    n_tiles = hid // tile
    hidden_shape = jax.ShapeDtypeStruct((per_dev, n, hid), jnp.bfloat16)
    whole = lambda *shape: pl.BlockSpec(shape, lambda l, f: (0,) * len(shape))
    col = lambda rows: pl.BlockSpec((1, rows, tile), lambda l, f: (l, 0, f))
    row = lambda cols: pl.BlockSpec((1, tile, cols), lambda l, f: (l, f, 0))
    per_expert = pl.BlockSpec((1, n, width), lambda l, f: (l, 0, 0))
    x, c, d_gate, d_up, hidden, back, gain_part, squares = pl.pallas_call(
        functools.partial(expert_kernel, n_tiles),
        grid=(per_dev, n_tiles),
        out_shape=(
            jax.ShapeDtypeStruct((n, width), jnp.bfloat16),
            jax.ShapeDtypeStruct((per_dev, n, width), jnp.bfloat16),
            hidden_shape,
            hidden_shape,
            hidden_shape,
            jax.ShapeDtypeStruct((n_dp, n_expert, width), jnp.float32),
            jax.ShapeDtypeStruct((1, width), jnp.float32),
            jax.ShapeDtypeStruct((1, 128), jnp.float32),
        ),
        in_specs=[
            whole(n, width),
            whole(n, width),
            whole(n, 128),
            whole(1, width),
            col(width),
            col(width),
            row(width),
        ],
        out_specs=[
            whole(n, width),
            per_expert,
            col(n),
            col(n),
            col(n),
            whole(n_dp, n_expert, width),
            whole(1, width),
            whole(1, 128),
        ],
        scratch_shapes=[
            pltpu.VMEM((n, width), jnp.float32),
            pltpu.VMEM((n, n), jnp.float32),
            pltpu.VMEM((n, n), jnp.float32),
            pltpu.VMEM((n, width), jnp.float32),
        ],
        compiler_params=pltpu.CompilerParams(**big),
        name="expert_pass",
    )(
        res_all.reshape(n, width),
        grad_all.reshape(n, width),
        meta_all.reshape(n, 128),
        norm_gain[None],
        w_gate,
        w_up,
        w_down,
    )
    piece = width // n_dp
    param_total = float(3 * n_expert * per_dev * width * hid * n_dp + width)
    vec = lambda *shape: pltpu.VMEM(shape, jnp.float32)
    grad_residual, gain_update, scale = pl.pallas_call(
        functools.partial(reduce_kernel, n_dp, n_expert, param_total),
        out_shape=(
            jax.ShapeDtypeStruct((1, width), jnp.float32),
            jax.ShapeDtypeStruct((n_dp, 1, piece), jnp.float32),
            jax.ShapeDtypeStruct((1, 128), jnp.float32),
        ),
        in_specs=[VMEM] * 6,
        out_specs=[VMEM] * 3,
        scratch_shapes=[
            vec(n_dp, 1, piece + 128),
            vec(n_dp, 1, piece + 128),
            vec(n_expert, 1, piece + 128),
            vec(n_dp, 1, piece),
            vec(n_dp, n_expert, width),
            vec(n_expert, 1, width),
            vec(n_expert, 1, width),
            pltpu.SemaphoreType.DMA((5, most)),
            pltpu.SemaphoreType.DMA((5, most)),
        ],
        compiler_params=pltpu.CompilerParams(collective_id=1, has_side_effects=True),
        name="reduce_rows",
    )(gain_part, squares, back, meta_all, residual, norm_gain[None])
    gate_update, up_update, down_update = pl.pallas_call(
        update_kernel,
        grid=(per_dev, n_tiles),
        out_shape=(
            jax.ShapeDtypeStruct(w_gate.shape, jnp.bfloat16),
            jax.ShapeDtypeStruct(w_up.shape, jnp.bfloat16),
            jax.ShapeDtypeStruct(w_down.shape, jnp.bfloat16),
        ),
        in_specs=[
            whole(n, width),
            per_expert,
            col(n),
            col(n),
            col(n),
            whole(1, 128),
        ],
        out_specs=[col(width), col(width), row(width)],
        scratch_shapes=[pltpu.VMEM((width, n), jnp.bfloat16)],
        compiler_params=pltpu.CompilerParams(**big),
        name="update_pass",
    )(x, c, d_gate, d_up, hidden, scale)
    return (grad_residual, gain_update.reshape(width), gate_update, up_update, down_update)


def shards_for(mesh):
    n_dp, n_expert = mesh.shape["dp"], mesh.shape["expert"]

    def run(*args):
        residual, w_gate = args[0], args[2]
        width, hid = w_gate.shape[1:]
        n = n_dp * n_expert
        fits = residual.shape[0] == 1 and hid % 128 == 0 and n <= 64 and width % (128 * n_dp) == 0
        if fits:
            return shards_kernel(n_dp, n_expert, *args)
        return shards_plain(*args)

    return run


def solution(mesh):
    placed = (
        P(("dp", "expert"), None),
        P(),
        P("expert", None, "dp"),
        P("expert", None, "dp"),
        P("expert", "dp", None),
        P(("dp", "expert"), None),
        P(("dp", "expert"), None),
        P(("dp", "expert")),
        P("dp"),
        P(("dp", "expert"), None),
    )
    return jax.shard_map(
        shards_for(mesh),
        mesh=mesh,
        in_specs=placed,
        out_specs=(
            P(("dp", "expert"), None),
            P(),
            P("expert", None, "dp"),
            P("expert", None, "dp"),
            P("expert", "dp", None),
        ),
        check_vma=False,
    )
```
